32 devices in a mesh: cell: 2 (over x), occ: 16 (over z, y, core).
Axes of the slice: x: 2, y: 2, z: 4, core: 2. Of those that a mesh axis runs over, the one named last changes fastest.
Arguments:
- factors: bfloat16 [12288, 16, 512], P('cell', 'occ'), parts along dimension 0, may hold values from -1.02 to 1.02
- gap_index: int32 [32, 512], P('cell'), parts along dimension 0, may hold values from 0 to 63
- gap_table: float32 [128], P('cell'), parts along dimension 0, may hold values from 0.25 to 2
- pair_level: int32 [32, 1], P('cell'), parts along dimension 0, may hold values from 0 to 7
- pair_shift: float32 [8], replicated, may hold values from 0.5 to 4
Outputs:
- gradient_factors: bfloat16 [12288, 16, 512], P('cell', 'occ'), parts along dimension 0
- pair_energy: float32 [2], P('cell'), parts along dimension 0
The draws below stay inside these ranges and needn't reach their ends.
There are 2 independent parts, one for each index of `cell`. The reference program is written for one: setup_inputs(seed, part) draws one part's arguments, and reference() takes and returns one part's arrays. A program takes and returns all parts, laid end to end along the dimension named above; an argument that names none is the same for every part. Nothing has to cross between parts.
All inputs are finite; a program needn't handle non-finite values.
Results may differ from the reference program's by a relative error of at most 0.0053.
Values may be sent and summed in bfloat16 or wider, within the bound.
A program may use at most 128 MiB of HBM per device.

```python
import math
import jax
import jax.numpy as jnp
from jax import lax

AUX = 6144
V = 512
OCC_DEV = 1
STEPS = 1
GAPS = 64
LEVELS = 8
BLOCKS = 16
NOCC = 16


def draw_factors(key, part):
    key_values = jax.random.fold_in(key, 11)
    block_ids = jnp.arange(NOCC) // OCC_DEV
    ramp = 0.75 + 0.6 * block_ids.astype(jnp.float32) / max(BLOCKS - 1, 1)
    values = jnp.clip(jax.random.normal(key_values, (AUX, NOCC, V), jnp.float32), -6.0, 6.0)
    return (0.125 * values * ramp[None, :, None]).astype(jnp.bfloat16)


def touch_ends(drawn, own_key, smallest, top_value):
    longest = drawn.shape.index(max(drawn.shape))
    spots = []
    for shift in (0, 1):
        where = [jax.random.randint(jax.random.fold_in(own_key, axis), (), 0, length) for axis, length in enumerate(drawn.shape)]
        where[longest] = (where[longest] + shift) % drawn.shape[longest]
        spots.append(tuple(where))
    return drawn.at[spots[0]].set(smallest).at[spots[1]].set(top_value)


def setup_inputs(seed: int = 0, part: int = 0) -> dict:
    key_of = jax.random.split(jax.random.key(seed), 6)
    part_splits = jax.random.split(jax.random.fold_in(key_of[5], part), 6)
    return {
        "factors": draw_factors(jax.random.fold_in(jax.random.fold_in(key_of[5], part), 71), part),
        "gap_index": touch_ends(jax.random.randint(part_splits[1], (NOCC, V), 0, GAPS), jax.random.fold_in(part_splits[1], 1), 0, GAPS - 1).astype(jnp.int32),
        "gap_table": jnp.clip(jnp.exp(jax.random.uniform(part_splits[2], (GAPS,), jnp.float32, math.log(0.25), math.log(2.0))), 0.25, 2.0),
        "pair_level": touch_ends(jax.random.randint(part_splits[3], (BLOCKS, STEPS), 0, LEVELS), jax.random.fold_in(part_splits[3], 1), 0, LEVELS - 1).astype(jnp.int32),
        "pair_shift": jnp.clip(jnp.exp(jax.random.uniform(key_of[4], (LEVELS,), jnp.float32, math.log(0.5), math.log(4.0))), 0.5, 4.0),
    }


def pair_terms(operands):
    own_block, partner, own_gap, partner_gap, shift_value = operands
    pairs = lax.dot_general(own_block, partner, (((0,), (0,)), ((), ())), preferred_element_type=jnp.float32)
    amplitude = pairs / (own_gap[:, None] + partner_gap[None, :] + shift_value)
    energy = jnp.sum(amplitude * pairs)
    amp_low = amplitude.astype(jnp.bfloat16)
    nearer = lax.dot_general(partner, amp_low, (((1,), (1,)), ((), ())), preferred_element_type=jnp.float32)
    farther = jnp.dot(own_block, amp_low, preferred_element_type=jnp.float32).astype(jnp.bfloat16)
    return nearer, farther, energy


def reference(factors, gap_index, gap_table, pair_level, pair_shift):
    columns = OCC_DEV * V
    blocks = jnp.transpose(factors.reshape(AUX, BLOCKS, columns), (1, 0, 2))
    gaps = gap_table[gap_index].reshape(BLOCKS, columns)
    gradient = jnp.zeros((BLOCKS, AUX, columns), jnp.float32)
    energy = jnp.zeros((), jnp.float32)
    for cycle_step in range(STEPS):
        distance = cycle_step + 1
        partners = jnp.roll(blocks, distance, axis=0)
        partner_gaps = jnp.roll(gaps, distance, axis=0)
        shifts = pair_shift[pair_level[:, cycle_step]]
        nearer, farther, sums = lax.map(pair_terms, (blocks, partners, gaps, partner_gaps, shifts))
        farther = lax.optimization_barrier(farther).astype(jnp.float32)
        gradient = gradient + nearer + jnp.roll(farther, -distance, axis=0)
        energy = energy + jnp.sum(sums)
    gradient_factors = jnp.transpose(gradient, (1, 0, 2)).reshape(AUX, NOCC, V).astype(jnp.bfloat16)
    pair_energy = (energy * (-1.3 / (BLOCKS * STEPS * columns * columns))).reshape(1)
    return gradient_factors, pair_energy
```

```python
import functools

import jax
import jax.numpy as jnp
from jax import lax
from jax.experimental import pallas as pl
from jax.experimental.pallas import tpu as pltpu
from jax.sharding import PartitionSpec as P

STEPS = 1
MESH = pl.DeviceIdType.MESH
CHUNK_ROWS = 128


def chunk_rows_of(aux_rows):
    rows = min(CHUNK_ROWS, aux_rows)
    while aux_rows % rows:
        rows -= 16
    return rows


def kernel(
    blocks, rows, scale,
    f_ref, index_ref, table_ref, level_ref, shift_ref,
    out_ref, energy_ref,
    own, visiting, outgoing, incoming, nearer, pairs, inverse, amp, gap_rows,
    energy_out, energy_in,
    own_sem, index_sem, f_send, f_recv, w_send, w_recv, e_send, e_recv,
):
    aux_rows, columns = own.shape
    chunks = aux_rows // rows
    me = lax.axis_index("occ")
    right = lax.rem(me + 1, blocks)
    left = lax.rem(me + blocks - 1, blocks)

    own_copy = pltpu.make_async_copy(f_ref, own, own_sem)
    own_copy.start()
    index_copy = pltpu.make_async_copy(index_ref, gap_rows, index_sem)
    index_copy.start()

    barrier = pltpu.get_barrier_semaphore()

    def greet(step, carry):
        other = lax.rem(me + step, blocks)
        pl.semaphore_signal(barrier, inc=1, device_id={"occ": other}, device_id_type=MESH)
        return carry

    lax.fori_loop(1, blocks, greet, 0)
    pl.semaphore_wait(barrier, blocks - 1)

    def rows_of(step):
        return pl.ds(pl.multiple_of(step * rows, rows), rows)

    def f_copy(step):
        return pltpu.make_async_remote_copy(
            src_ref=f_ref.at[rows_of(step)], dst_ref=visiting.at[rows_of(step)],
            send_sem=f_send.at[step], recv_sem=f_recv.at[step],
            device_id={"occ": right}, device_id_type=MESH,
        )

    def w_copy(step):
        return pltpu.make_async_remote_copy(
            src_ref=outgoing.at[rows_of(step)], dst_ref=incoming.at[rows_of(step)],
            send_sem=w_send.at[step], recv_sem=w_recv.at[step],
            device_id={"occ": left}, device_id_type=MESH,
        )

    def e_copy(source, target):
        return pltpu.make_async_remote_copy(
            src_ref=energy_out.at[pl.ds(0, 1)], dst_ref=energy_in.at[source, pl.ds(0, 1)],
            send_sem=e_send.at[target], recv_sem=e_recv.at[source],
            device_id={"occ": target}, device_id_type=MESH,
        )

    @pl.loop(0, chunks)
    def _(step):
        f_copy(step).start()

    index_copy.wait()
    own_index = gap_rows[pl.ds(me, 1), :]
    partner_index = gap_rows[pl.ds(left, 1), :]
    zeros = jnp.zeros((1, columns), jnp.float32)

    def look_up(entry, gaps):
        value = table_ref[entry]
        return (
            jnp.where(own_index == entry, value, gaps[0]),
            jnp.where(partner_index == entry, value, gaps[1]),
        )

    own_gap, partner_gap = lax.fori_loop(0, table_ref.shape[0], look_up, (zeros, zeros))
    level = level_ref[me]
    shift = jnp.float32(0.0)
    for entry in range(shift_ref.shape[0]):
        shift = jnp.where(level == entry, shift_ref[entry], shift)
    own_column = jnp.transpose(jnp.broadcast_to(own_gap, (128, columns)))
    for start in range(0, columns, 128):
        part = pl.ds(start, 128)
        inverse[:, part] = 1.0 / (own_column + partner_gap[:, start : start + 128] + shift)

    pairs[...] = jnp.zeros_like(pairs)
    own_copy.wait()

    @pl.loop(0, chunks)
    def _(step):
        f_copy(step).wait_recv()
        pairs[...] += lax.dot_general(
            own[rows_of(step), :], visiting[rows_of(step), :], (((0,), (0,)), ((), ())),
            preferred_element_type=jnp.float32,
        )

    amp[...] = (pairs[...] * inverse[...]).astype(jnp.bfloat16)

    def send_w(step):
        outgoing[rows_of(step), :] = jnp.dot(
            own[rows_of(step), :], amp[...], preferred_element_type=jnp.float32
        ).astype(jnp.bfloat16)
        w_copy(step).start()

    send_w(0)
    pair = pairs[...]
    total = jnp.sum(pair * pair * inverse[...])
    energy_out[...] = jnp.full(energy_out.shape, total, jnp.float32)
    energy_in[me] = jnp.full(energy_out.shape, total, jnp.float32)

    @pl.loop(1, blocks)
    def _(step):
        e_copy(me, lax.rem(me + step, blocks)).start()

    @pl.loop(1, chunks)
    def _(step):
        send_w(step)

    @pl.loop(0, chunks)
    def _(step):
        nearer[rows_of(step), :] = lax.dot_general(
            visiting[rows_of(step), :], amp[...], (((1,), (1,)), ((), ())),
            preferred_element_type=jnp.float32,
        )

    @pl.loop(1, blocks)
    def _(step):
        e_copy(lax.rem(me + step, blocks), lax.rem(me + step, blocks)).wait_recv()

    energy_sum = energy_in[0]
    for block in range(1, blocks):
        energy_sum = energy_sum + energy_in[block]
    energy_ref[0] = energy_sum[0, 0] * scale

    @pl.loop(0, chunks)
    def _(step):
        f_copy(step).wait_send()

    @pl.loop(1, blocks)
    def _(step):
        e_copy(me, lax.rem(me + step, blocks)).wait_send()

    @pl.loop(0, chunks)
    def _(step):
        w_copy(step).wait_recv()
        out_ref[rows_of(step), :] = (
            nearer[rows_of(step), :] + incoming[rows_of(step), :].astype(jnp.float32)
        ).astype(jnp.bfloat16)

    @pl.loop(0, chunks)
    def _(step):
        w_copy(step).wait_send()


def on_device(factors, gap_index, gap_table, pair_level, pair_shift):
    aux_rows, occ_count, virtuals = factors.shape
    columns = occ_count * virtuals
    blocks = lax.axis_size("occ")
    rows = chunk_rows_of(aux_rows)
    chunks = aux_rows // rows
    scale = -1.3 / (blocks * STEPS * columns * columns)
    gradient, pair_energy = pl.pallas_call(
        functools.partial(kernel, blocks, rows, scale),
        out_shape=(
            OUT_SPACE((aux_rows, columns), jnp.bfloat16),
            jax.ShapeDtypeStruct((1,), jnp.float32),
        ),
        in_specs=[
            pl.BlockSpec(memory_space=pl.ANY),
            pl.BlockSpec(memory_space=pl.ANY),
            pl.BlockSpec(memory_space=pltpu.SMEM),
            pl.BlockSpec(memory_space=pltpu.SMEM),
            pl.BlockSpec(memory_space=pltpu.SMEM),
        ],
        out_specs=(
            pl.BlockSpec(memory_space=pltpu.VMEM),
            pl.BlockSpec(memory_space=pltpu.SMEM),
        ),
        scratch_shapes=[
            pltpu.VMEM((aux_rows, columns), jnp.bfloat16),
            pltpu.VMEM((aux_rows, columns), jnp.bfloat16),
            pltpu.VMEM((aux_rows, columns), jnp.bfloat16),
            pltpu.VMEM((aux_rows, columns), jnp.bfloat16),
            pltpu.VMEM((aux_rows, columns), jnp.float32),
            pltpu.VMEM((columns, columns), jnp.float32),
            pltpu.VMEM((columns, columns), jnp.float32),
            pltpu.VMEM((columns, columns), jnp.bfloat16),
            pltpu.VMEM((blocks, columns), jnp.int32),
            pltpu.VMEM((8, 128), jnp.float32),
            pltpu.VMEM((blocks, 8, 128), jnp.float32),
            pltpu.SemaphoreType.DMA,
            pltpu.SemaphoreType.DMA,
            pltpu.SemaphoreType.DMA((chunks,)),
            pltpu.SemaphoreType.DMA((chunks,)),
            pltpu.SemaphoreType.DMA((chunks,)),
            pltpu.SemaphoreType.DMA((chunks,)),
            pltpu.SemaphoreType.DMA((blocks,)),
            pltpu.SemaphoreType.DMA((blocks,)),
        ],
        compiler_params=pltpu.CompilerParams(
            collective_id=0, has_side_effects=True, vmem_limit_bytes=56 * 1024 * 1024
        ),
    )(
        factors.reshape(aux_rows, columns),
        gap_index.reshape(blocks, columns),
        gap_table,
        pair_level.reshape(-1),
        pair_shift,
    )
    return gradient.reshape(aux_rows, occ_count, virtuals), pair_energy


OUT_SPACE = pltpu.VMEM


def solution(mesh):
    in_specs = (P("cell", "occ", None), P("cell", None), P("cell"), P("cell", None), P())
    out_specs = (P("cell", "occ", None), P("cell"))
    return jax.shard_map(
        on_device, mesh=mesh, in_specs=in_specs, out_specs=out_specs, check_vma=False
    )
```

```python
import functools

import jax
import jax.numpy as jnp
from jax import lax
from jax.experimental import pallas as pl
from jax.experimental.pallas import tpu as pltpu
from jax.sharding import PartitionSpec as P

STEPS = 1
MESH = pl.DeviceIdType.MESH
CHUNK_ROWS = 256
EARLY = 4


def chunk_rows_of(aux_rows):
    rows = min(CHUNK_ROWS, aux_rows)
    while aux_rows % rows:
        rows -= 16
    return rows


def part_columns_of(columns):
    return columns // 2 if columns % 256 == 0 else columns


def kernel(
    blocks, rows, width, scale,
    f_ref, index_ref, table_ref, level_ref, shift_ref,
    out_ref, energy_ref,
    own, visiting, outgoing, incoming, nearer, pairs, inverse, amp, gap_rows,
    energy_out, energy_in,
    own_sem, index_sem, f_send, f_recv, w_send, w_recv, e_send, e_recv,
):
    aux_rows, columns = own.shape
    chunks = aux_rows // rows
    me = lax.axis_index("occ")
    right = lax.rem(me + 1, blocks)
    left = lax.rem(me + blocks - 1, blocks)

    own_copy = pltpu.make_async_copy(f_ref, own, own_sem)
    own_copy.start()
    index_copy = pltpu.make_async_copy(index_ref, gap_rows, index_sem)
    index_copy.start()

    barrier = pltpu.get_barrier_semaphore()

    def greet(step, carry):
        other = lax.rem(me + step, blocks)
        pl.semaphore_signal(barrier, inc=1, device_id={"occ": other}, device_id_type=MESH)
        return carry

    lax.fori_loop(1, blocks, greet, 0)
    pl.semaphore_wait(barrier, blocks - 1)

    parts = columns // width

    def rows_of(step):
        return pl.ds(pl.multiple_of(step * rows, rows), rows)

    def columns_of(part):
        return pl.ds(part * width, width)

    def f_copy(part, step):
        return pltpu.make_async_remote_copy(
            src_ref=f_ref.at[rows_of(step), columns_of(part)],
            dst_ref=visiting.at[rows_of(step), columns_of(part)],
            send_sem=f_send.at[part, step], recv_sem=f_recv.at[part, step],
            device_id={"occ": right}, device_id_type=MESH,
        )

    def w_copy(part, step):
        return pltpu.make_async_remote_copy(
            src_ref=outgoing.at[rows_of(step), columns_of(part)],
            dst_ref=incoming.at[rows_of(step), columns_of(part)],
            send_sem=w_send.at[part, step], recv_sem=w_recv.at[part, step],
            device_id={"occ": left}, device_id_type=MESH,
        )

    def e_copy(source, target):
        return pltpu.make_async_remote_copy(
            src_ref=energy_out.at[pl.ds(0, 1)], dst_ref=energy_in.at[source, pl.ds(0, 1)],
            send_sem=e_send.at[target], recv_sem=e_recv.at[source],
            device_id={"occ": target}, device_id_type=MESH,
        )

    for part in range(parts):
        @pl.loop(0, chunks)
        def _(step):
            f_copy(part, step).start()

    index_copy.wait()
    own_index = gap_rows[pl.ds(me, 1), :]
    partner_index = gap_rows[pl.ds(left, 1), :]
    zeros = jnp.zeros((1, columns), jnp.float32)

    def look_up(entry, gaps):
        value = table_ref[entry]
        return (
            jnp.where(own_index == entry, value, gaps[0]),
            jnp.where(partner_index == entry, value, gaps[1]),
        )

    own_gap, partner_gap = lax.fori_loop(0, table_ref.shape[0], look_up, (zeros, zeros))
    level = level_ref[me]
    shift = jnp.float32(0.0)
    for entry in range(shift_ref.shape[0]):
        shift = jnp.where(level == entry, shift_ref[entry], shift)
    own_column = jnp.transpose(jnp.broadcast_to(own_gap, (128, columns)))
    for start in range(0, columns, 128):
        part = pl.ds(start, 128)
        inverse[:, part] = 1.0 / (own_column + partner_gap[:, start : start + 128] + shift)

    pairs[...] = jnp.zeros_like(pairs)
    own_copy.wait()

    def add_pairs(part, step):
        f_copy(part, step).wait_recv()
        pairs[:, columns_of(part)] += lax.dot_general(
            own[rows_of(step), :], visiting[rows_of(step), columns_of(part)], (((0,), (0,)), ((), ())),
            preferred_element_type=jnp.float32,
        )

    def form_amp(part):
        amp[:, columns_of(part)] = (
            pairs[:, columns_of(part)] * inverse[:, columns_of(part)]
        ).astype(jnp.bfloat16)

    def form_w(part, step):
        outgoing[rows_of(step), columns_of(part)] = jnp.dot(
            own[rows_of(step), :], amp[:, columns_of(part)], preferred_element_type=jnp.float32
        ).astype(jnp.bfloat16)

    for part in range(parts - 1):
        @pl.loop(0, chunks)
        def _(step):
            add_pairs(part, step)

        form_amp(part)

        @pl.loop(0, chunks)
        def _(step):
            form_w(part, step)

    last = parts - 1
    early = max(chunks - EARLY, 0)

    @pl.loop(0, early)
    def _(step):
        add_pairs(last, step)

    for part in range(last):
        @pl.loop(0, chunks)
        def _(step):
            w_copy(part, step).start()

    @pl.loop(early, chunks)
    def _(step):
        add_pairs(last, step)

    form_amp(last)

    def send_w(step):
        form_w(last, step)
        w_copy(last, step).start()

    send_w(0)
    pair = pairs[...]
    total = jnp.sum(pair * pair * inverse[...])
    energy_out[...] = jnp.full(energy_out.shape, total, jnp.float32)
    energy_in[me] = jnp.full(energy_out.shape, total, jnp.float32)

    @pl.loop(1, blocks)
    def _(step):
        e_copy(me, lax.rem(me + step, blocks)).start()

    @pl.loop(1, chunks)
    def _(step):
        send_w(step)

    @pl.loop(0, chunks)
    def _(step):
        nearer[rows_of(step), :] = lax.dot_general(
            visiting[rows_of(step), :], amp[...], (((1,), (1,)), ((), ())),
            preferred_element_type=jnp.float32,
        )

    @pl.loop(1, blocks)
    def _(step):
        e_copy(lax.rem(me + step, blocks), lax.rem(me + step, blocks)).wait_recv()

    energy_sum = energy_in[0]
    for block in range(1, blocks):
        energy_sum = energy_sum + energy_in[block]
    energy_ref[0] = energy_sum[0, 0] * scale

    for part in range(parts):
        @pl.loop(0, chunks)
        def _(step):
            f_copy(part, step).wait_send()

    @pl.loop(1, blocks)
    def _(step):
        e_copy(me, lax.rem(me + step, blocks)).wait_send()

    for part in range(parts):
        @pl.loop(0, chunks)
        def _(step):
            w_copy(part, step).wait_recv()
            out_ref[rows_of(step), columns_of(part)] = (
                nearer[rows_of(step), columns_of(part)]
                + incoming[rows_of(step), columns_of(part)].astype(jnp.float32)
            ).astype(jnp.bfloat16)

    for part in range(parts):
        @pl.loop(0, chunks)
        def _(step):
            w_copy(part, step).wait_send()


def on_device(factors, gap_index, gap_table, pair_level, pair_shift):
    aux_rows, occ_count, virtuals = factors.shape
    columns = occ_count * virtuals
    blocks = lax.axis_size("occ")
    rows = chunk_rows_of(aux_rows)
    chunks = aux_rows // rows
    width = part_columns_of(columns)
    parts = columns // width
    scale = -1.3 / (blocks * STEPS * columns * columns)
    gradient, pair_energy = pl.pallas_call(
        functools.partial(kernel, blocks, rows, width, scale),
        out_shape=(
            OUT_SPACE((aux_rows, columns), jnp.bfloat16),
            jax.ShapeDtypeStruct((1,), jnp.float32),
        ),
        in_specs=[
            pl.BlockSpec(memory_space=pl.ANY),
            pl.BlockSpec(memory_space=pl.ANY),
            pl.BlockSpec(memory_space=pltpu.SMEM),
            pl.BlockSpec(memory_space=pltpu.SMEM),
            pl.BlockSpec(memory_space=pltpu.SMEM),
        ],
        out_specs=(
            pl.BlockSpec(memory_space=pltpu.VMEM),
            pl.BlockSpec(memory_space=pltpu.SMEM),
        ),
        scratch_shapes=[
            pltpu.VMEM((aux_rows, columns), jnp.bfloat16),
            pltpu.VMEM((aux_rows, columns), jnp.bfloat16),
            pltpu.VMEM((aux_rows, columns), jnp.bfloat16),
            pltpu.VMEM((aux_rows, columns), jnp.bfloat16),
            pltpu.VMEM((aux_rows, columns), jnp.float32),
            pltpu.VMEM((columns, columns), jnp.float32),
            pltpu.VMEM((columns, columns), jnp.float32),
            pltpu.VMEM((columns, columns), jnp.bfloat16),
            pltpu.VMEM((blocks, columns), jnp.int32),
            pltpu.VMEM((8, 128), jnp.float32),
            pltpu.VMEM((blocks, 8, 128), jnp.float32),
            pltpu.SemaphoreType.DMA,
            pltpu.SemaphoreType.DMA,
            pltpu.SemaphoreType.DMA((parts, chunks)),
            pltpu.SemaphoreType.DMA((parts, chunks)),
            pltpu.SemaphoreType.DMA((parts, chunks)),
            pltpu.SemaphoreType.DMA((parts, chunks)),
            pltpu.SemaphoreType.DMA((blocks,)),
            pltpu.SemaphoreType.DMA((blocks,)),
        ],
        compiler_params=pltpu.CompilerParams(
            collective_id=0, has_side_effects=True, vmem_limit_bytes=56 * 1024 * 1024
        ),
    )(
        factors.reshape(aux_rows, columns),
        gap_index.reshape(blocks, columns),
        gap_table,
        pair_level.reshape(-1),
        pair_shift,
    )
    return gradient.reshape(aux_rows, occ_count, virtuals), pair_energy


OUT_SPACE = pltpu.VMEM


def solution(mesh):
    in_specs = (P("cell", "occ", None), P("cell", None), P("cell"), P("cell", None), P())
    out_specs = (P("cell", "occ", None), P("cell"))
    return jax.shard_map(
        on_device, mesh=mesh, in_specs=in_specs, out_specs=out_specs, check_vma=False
    )
```

```python
import functools

import jax
import jax.numpy as jnp
from jax import lax
from jax.experimental import pallas as pl
from jax.experimental.pallas import tpu as pltpu
from jax.sharding import PartitionSpec as P

STEPS = 1
MESH = pl.DeviceIdType.MESH
CHUNK_ROWS = 512
EARLY = 2
IN_FLIGHT = 0


def chunk_rows_of(aux_rows):
    rows = min(CHUNK_ROWS, aux_rows)
    while aux_rows % rows:
        rows -= 16
    return rows


def part_columns_of(columns):
    return columns // 2 if columns % 256 == 0 else columns


def stages_of(blocks):
    stages = 0
    while 2**stages < blocks // 2:
        stages += 1
    return stages


def kernel(
    blocks, rows, width, scale,
    f_ref, index_ref, table_ref, level_ref, shift_ref,
    out_ref, energy_ref,
    own, visiting, outgoing, incoming, nearer, pairs, inverse, amp, gap_rows,
    energy_out, energy_in,
    own_sem, index_sem, f_send, f_recv, w_send, w_recv, e_send, e_recv, f_left, started,
):
    aux_rows, columns = own.shape
    chunks = aux_rows // rows
    me = lax.axis_index("occ")
    right = lax.rem(me + 1, blocks)
    left = lax.rem(me + blocks - 1, blocks)

    own_copy = pltpu.make_async_copy(f_ref, own, own_sem)
    own_copy.start()
    index_copy = pltpu.make_async_copy(index_ref, gap_rows, index_sem)
    index_copy.start()

    barrier = pltpu.get_barrier_semaphore()

    for other in (left, right):
        pl.semaphore_signal(barrier, inc=1, device_id={"occ": other}, device_id_type=MESH)
    pl.semaphore_wait(barrier, 2)

    parts = columns // width

    def rows_of(step):
        return pl.ds(pl.multiple_of(step * rows, rows), rows)

    def columns_of(part):
        return pl.ds(part * width, width)

    def f_copy(part, step):
        return pltpu.make_async_remote_copy(
            src_ref=f_ref.at[rows_of(step), columns_of(part)],
            dst_ref=visiting.at[rows_of(step), columns_of(part)],
            send_sem=f_send.at[part, step], recv_sem=f_recv.at[part, step],
            device_id={"occ": right}, device_id_type=MESH,
        )

    def w_copy(part, step):
        return pltpu.make_async_remote_copy(
            src_ref=outgoing.at[rows_of(step), columns_of(part)],
            dst_ref=incoming.at[rows_of(step), columns_of(part)],
            send_sem=w_send.at[part, step], recv_sem=w_recv.at[part, step],
            device_id={"occ": left}, device_id_type=MESH,
        )

    def e_copy(source, target):
        return pltpu.make_async_remote_copy(
            src_ref=energy_out.at[pl.ds(0, 1)], dst_ref=energy_in.at[source, pl.ds(0, 1)],
            send_sem=e_send.at[target], recv_sem=e_recv.at[source],
            device_id={"occ": target}, device_id_type=MESH,
        )

    for part in range(parts):
        @pl.loop(0, chunks)
        def _(step):
            f_copy(part, step).start()

    index_copy.wait()
    own_index = gap_rows[pl.ds(me, 1), :]
    partner_index = gap_rows[pl.ds(left, 1), :]
    zeros = jnp.zeros((1, columns), jnp.float32)

    def look_up(entry, gaps):
        value = table_ref[entry]
        return (
            jnp.where(own_index == entry, value, gaps[0]),
            jnp.where(partner_index == entry, value, gaps[1]),
        )

    own_gap, partner_gap = lax.fori_loop(0, table_ref.shape[0], look_up, (zeros, zeros))
    level = level_ref[me]
    shift = jnp.float32(0.0)
    for entry in range(shift_ref.shape[0]):
        shift = jnp.where(level == entry, shift_ref[entry], shift)
    own_column = jnp.transpose(jnp.broadcast_to(own_gap, (128, columns)))
    for start in range(0, columns, 128):
        part = pl.ds(start, 128)
        inverse[:, part] = 1.0 / (own_column + partner_gap[:, start : start + 128] + shift)

    pairs[...] = jnp.zeros_like(pairs)
    own_copy.wait()

    for stage in range(stages_of(blocks)):
        reach = 2**stage
        for other in (lax.rem(me + reach, blocks), lax.rem(me + blocks - reach, blocks)):
            pl.semaphore_signal(started.at[stage], inc=1, device_id={"occ": other}, device_id_type=MESH)
        pl.semaphore_wait(started.at[stage], 2)

    def add_pairs(part, step):
        f_copy(part, step).wait_recv()
        pairs[:, columns_of(part)] += lax.dot_general(
            own[rows_of(step), :], visiting[rows_of(step), columns_of(part)], (((0,), (0,)), ((), ())),
            preferred_element_type=jnp.float32,
        )

    def form_amp(part):
        amp[:, columns_of(part)] = (
            pairs[:, columns_of(part)] * inverse[:, columns_of(part)]
        ).astype(jnp.bfloat16)

    def form_w(part, step):
        outgoing[rows_of(step), columns_of(part)] = jnp.dot(
            own[rows_of(step), :], amp[:, columns_of(part)], preferred_element_type=jnp.float32
        ).astype(jnp.bfloat16)

    for part in range(parts - 1):
        @pl.loop(0, chunks)
        def _(step):
            add_pairs(part, step)

        form_amp(part)

        @pl.loop(0, chunks)
        def _(step):
            form_w(part, step)

    last = parts - 1
    early = max(chunks - EARLY, 0)
    in_flight = min(IN_FLIGHT, chunks)

    @pl.loop(0, early)
    def _(step):
        add_pairs(last, step)

    for part in range(parts):
        @pl.loop(0, chunks if part < last else chunks - in_flight)
        def _(step):
            f_copy(part, step).wait_send()

    pl.semaphore_signal(f_left, inc=1, device_id={"occ": left}, device_id_type=MESH)
    pl.semaphore_wait(f_left, 1)

    for part in range(last):
        @pl.loop(0, chunks)
        def _(step):
            w_copy(part, step).start()

    @pl.loop(early, chunks)
    def _(step):
        add_pairs(last, step)

    form_amp(last)

    def send_w(step):
        form_w(last, step)
        w_copy(last, step).start()

    send_w(0)
    pair = pairs[...]
    total = jnp.sum(pair * pair * inverse[...])
    energy_out[...] = jnp.full(energy_out.shape, total, jnp.float32)
    energy_in[me] = jnp.full(energy_out.shape, total, jnp.float32)

    @pl.loop(1, blocks)
    def _(step):
        e_copy(me, lax.rem(me + step, blocks)).start()

    @pl.loop(1, chunks)
    def _(step):
        send_w(step)

    @pl.loop(0, chunks)
    def _(step):
        nearer[rows_of(step), :] = lax.dot_general(
            visiting[rows_of(step), :], amp[...], (((1,), (1,)), ((), ())),
            preferred_element_type=jnp.float32,
        )

    @pl.loop(1, blocks)
    def _(step):
        e_copy(lax.rem(me + step, blocks), lax.rem(me + step, blocks)).wait_recv()

    energy_sum = energy_in[0]
    for block in range(1, blocks):
        energy_sum = energy_sum + energy_in[block]
    energy_ref[0] = energy_sum[0, 0] * scale

    @pl.loop(chunks - in_flight, chunks)
    def _(step):
        f_copy(last, step).wait_send()

    @pl.loop(1, blocks)
    def _(step):
        e_copy(me, lax.rem(me + step, blocks)).wait_send()

    for part in range(parts):
        @pl.loop(0, chunks)
        def _(step):
            w_copy(part, step).wait_recv()
            out_ref[rows_of(step), columns_of(part)] = (
                nearer[rows_of(step), columns_of(part)]
                + incoming[rows_of(step), columns_of(part)].astype(jnp.float32)
            ).astype(jnp.bfloat16)

    for part in range(parts):
        @pl.loop(0, chunks)
        def _(step):
            w_copy(part, step).wait_send()


def on_device(factors, gap_index, gap_table, pair_level, pair_shift):
    aux_rows, occ_count, virtuals = factors.shape
    columns = occ_count * virtuals
    blocks = lax.axis_size("occ")
    rows = chunk_rows_of(aux_rows)
    chunks = aux_rows // rows
    width = part_columns_of(columns)
    parts = columns // width
    scale = -1.3 / (blocks * STEPS * columns * columns)
    gradient, pair_energy = pl.pallas_call(
        functools.partial(kernel, blocks, rows, width, scale),
        out_shape=(
            OUT_SPACE((aux_rows, columns), jnp.bfloat16),
            jax.ShapeDtypeStruct((1,), jnp.float32),
        ),
        in_specs=[
            pl.BlockSpec(memory_space=pl.ANY),
            pl.BlockSpec(memory_space=pl.ANY),
            pl.BlockSpec(memory_space=pltpu.SMEM),
            pl.BlockSpec(memory_space=pltpu.SMEM),
            pl.BlockSpec(memory_space=pltpu.SMEM),
        ],
        out_specs=(
            pl.BlockSpec(memory_space=pltpu.VMEM),
            pl.BlockSpec(memory_space=pltpu.SMEM),
        ),
        scratch_shapes=[
            pltpu.VMEM((aux_rows, columns), jnp.bfloat16),
            pltpu.VMEM((aux_rows, columns), jnp.bfloat16),
            pltpu.VMEM((aux_rows, columns), jnp.bfloat16),
            pltpu.VMEM((aux_rows, columns), jnp.bfloat16),
            pltpu.VMEM((aux_rows, columns), jnp.float32),
            pltpu.VMEM((columns, columns), jnp.float32),
            pltpu.VMEM((columns, columns), jnp.float32),
            pltpu.VMEM((columns, columns), jnp.bfloat16),
            pltpu.VMEM((blocks, columns), jnp.int32),
            pltpu.VMEM((8, 128), jnp.float32),
            pltpu.VMEM((blocks, 8, 128), jnp.float32),
            pltpu.SemaphoreType.DMA,
            pltpu.SemaphoreType.DMA,
            pltpu.SemaphoreType.DMA((parts, chunks)),
            pltpu.SemaphoreType.DMA((parts, chunks)),
            pltpu.SemaphoreType.DMA((parts, chunks)),
            pltpu.SemaphoreType.DMA((parts, chunks)),
            pltpu.SemaphoreType.DMA((blocks,)),
            pltpu.SemaphoreType.DMA((blocks,)),
            pltpu.SemaphoreType.REGULAR,
            pltpu.SemaphoreType.REGULAR((max(stages_of(blocks), 1),)),
        ],
        compiler_params=pltpu.CompilerParams(
            collective_id=0, has_side_effects=True, vmem_limit_bytes=56 * 1024 * 1024
        ),
    )(
        factors.reshape(aux_rows, columns),
        gap_index.reshape(blocks, columns),
        gap_table,
        pair_level.reshape(-1),
        pair_shift,
    )
    return gradient.reshape(aux_rows, occ_count, virtuals), pair_energy


OUT_SPACE = pltpu.VMEM


def solution(mesh):
    in_specs = (P("cell", "occ", None), P("cell", None), P("cell"), P("cell", None), P())
    out_specs = (P("cell", "occ", None), P("cell"))
    return jax.shard_map(
        on_device, mesh=mesh, in_specs=in_specs, out_specs=out_specs, check_vma=False
    )
```

```python
import functools

import jax
import jax.numpy as jnp
from jax import lax
from jax.experimental import pallas as pl
from jax.experimental.pallas import tpu as pltpu
from jax.sharding import PartitionSpec as P

STEPS = 1
MESH = pl.DeviceIdType.MESH
CHUNK_ROWS = 1024
EARLY = 2
IN_FLIGHT = 0


def chunk_rows_of(aux_rows):
    rows = min(CHUNK_ROWS, aux_rows)
    while aux_rows % rows:
        rows -= 16
    return rows


def part_columns_of(columns):
    return columns // 2 if columns % 256 == 0 else columns


def stages_of(blocks):
    stages = 0
    while 2**stages < blocks // 2:
        stages += 1
    return stages


def kernel(
    blocks, rows, width, scale,
    f_ref, index_ref, table_ref, level_ref, shift_ref,
    out_ref, energy_ref,
    own, visiting, outgoing, incoming, nearer, pairs, inverse, amp, gap_rows,
    energy_out, energy_in,
    own_sem, index_sem, f_send, f_recv, w_send, w_recv, e_send, e_recv, f_left, started,
):
    aux_rows, columns = own.shape
    chunks = aux_rows // rows
    me = lax.axis_index("occ")
    right = lax.rem(me + 1, blocks)
    left = lax.rem(me + blocks - 1, blocks)

    own_copy = pltpu.make_async_copy(f_ref, own, own_sem)
    own_copy.start()
    index_copy = pltpu.make_async_copy(index_ref, gap_rows, index_sem)
    index_copy.start()

    barrier = pltpu.get_barrier_semaphore()

    for other in (left, right):
        pl.semaphore_signal(barrier, inc=1, device_id={"occ": other}, device_id_type=MESH)
    pl.semaphore_wait(barrier, 2)

    parts = columns // width

    def rows_of(step):
        return pl.ds(pl.multiple_of(step * rows, rows), rows)

    def columns_of(part):
        return pl.ds(part * width, width)

    def f_copy(part, step):
        return pltpu.make_async_remote_copy(
            src_ref=f_ref.at[rows_of(step), columns_of(part)],
            dst_ref=visiting.at[rows_of(step), columns_of(part)],
            send_sem=f_send.at[part, step], recv_sem=f_recv.at[part, step],
            device_id={"occ": right}, device_id_type=MESH,
        )

    def w_copy(part, step):
        return pltpu.make_async_remote_copy(
            src_ref=outgoing.at[rows_of(step), columns_of(part)],
            dst_ref=incoming.at[rows_of(step), columns_of(part)],
            send_sem=w_send.at[part, step], recv_sem=w_recv.at[part, step],
            device_id={"occ": left}, device_id_type=MESH,
        )

    def e_copy(source, target):
        return pltpu.make_async_remote_copy(
            src_ref=energy_out.at[pl.ds(0, 1)], dst_ref=energy_in.at[source, pl.ds(0, 1)],
            send_sem=e_send.at[target], recv_sem=e_recv.at[source],
            device_id={"occ": target}, device_id_type=MESH,
        )

    for part in range(parts):
        @pl.loop(0, chunks)
        def _(step):
            f_copy(part, step).start()

    index_copy.wait()
    own_index = gap_rows[pl.ds(me, 1), :]
    partner_index = gap_rows[pl.ds(left, 1), :]
    zeros = jnp.zeros((1, columns), jnp.float32)

    def look_up(entry, gaps):
        value = table_ref[entry]
        return (
            jnp.where(own_index == entry, value, gaps[0]),
            jnp.where(partner_index == entry, value, gaps[1]),
        )

    own_gap, partner_gap = lax.fori_loop(0, table_ref.shape[0], look_up, (zeros, zeros))
    level = level_ref[me]
    shift = jnp.float32(0.0)
    for entry in range(shift_ref.shape[0]):
        shift = jnp.where(level == entry, shift_ref[entry], shift)
    own_column = jnp.transpose(jnp.broadcast_to(own_gap, (128, columns)))
    for start in range(0, columns, 128):
        part = pl.ds(start, 128)
        inverse[:, part] = 1.0 / (own_column + partner_gap[:, start : start + 128] + shift)

    pairs[...] = jnp.zeros_like(pairs)
    own_copy.wait()

    for stage in range(stages_of(blocks)):
        reach = 2**stage
        for other in (lax.rem(me + reach, blocks), lax.rem(me + blocks - reach, blocks)):
            pl.semaphore_signal(started.at[stage], inc=1, device_id={"occ": other}, device_id_type=MESH)
        pl.semaphore_wait(started.at[stage], 2)

    def add_pairs(part, step):
        f_copy(part, step).wait_recv()
        pairs[:, columns_of(part)] += lax.dot_general(
            own[rows_of(step), :], visiting[rows_of(step), columns_of(part)], (((0,), (0,)), ((), ())),
            preferred_element_type=jnp.float32,
        )

    def form_amp(part):
        amp[:, columns_of(part)] = (
            pairs[:, columns_of(part)] * inverse[:, columns_of(part)]
        ).astype(jnp.bfloat16)

    def form_w(part, step):
        outgoing[rows_of(step), columns_of(part)] = jnp.dot(
            own[rows_of(step), :], amp[:, columns_of(part)], preferred_element_type=jnp.float32
        ).astype(jnp.bfloat16)

    for part in range(parts - 1):
        @pl.loop(0, chunks)
        def _(step):
            add_pairs(part, step)

        form_amp(part)

        @pl.loop(0, chunks)
        def _(step):
            form_w(part, step)

    last = parts - 1
    early = max(chunks - EARLY, 0)
    in_flight = min(IN_FLIGHT, chunks)

    @pl.loop(0, early)
    def _(step):
        add_pairs(last, step)

    for part in range(parts):
        @pl.loop(0, chunks if part < last else chunks - in_flight)
        def _(step):
            f_copy(part, step).wait_send()

    pl.semaphore_signal(f_left, inc=1, device_id={"occ": left}, device_id_type=MESH)
    pl.semaphore_wait(f_left, 1)

    for part in range(last):
        @pl.loop(0, chunks)
        def _(step):
            w_copy(part, step).start()

    @pl.loop(early, chunks)
    def _(step):
        add_pairs(last, step)

    form_amp(last)

    def send_w(step):
        form_w(last, step)
        w_copy(last, step).start()

    send_w(0)
    pair = pairs[...]
    total = jnp.sum(pair * pair * inverse[...])
    energy_out[...] = jnp.full(energy_out.shape, total, jnp.float32)
    energy_in[me] = jnp.full(energy_out.shape, total, jnp.float32)

    @pl.loop(1, blocks)
    def _(step):
        e_copy(me, lax.rem(me + step, blocks)).start()

    @pl.loop(1, chunks)
    def _(step):
        send_w(step)

    @pl.loop(0, chunks)
    def _(step):
        nearer[rows_of(step), :] = lax.dot_general(
            visiting[rows_of(step), :], amp[...], (((1,), (1,)), ((), ())),
            preferred_element_type=jnp.float32,
        )

    @pl.loop(1, blocks)
    def _(step):
        e_copy(lax.rem(me + step, blocks), lax.rem(me + step, blocks)).wait_recv()

    energy_sum = energy_in[0]
    for block in range(1, blocks):
        energy_sum = energy_sum + energy_in[block]
    energy_ref[0] = energy_sum[0, 0] * scale

    @pl.loop(chunks - in_flight, chunks)
    def _(step):
        f_copy(last, step).wait_send()

    @pl.loop(1, blocks)
    def _(step):
        e_copy(me, lax.rem(me + step, blocks)).wait_send()

    for part in range(parts):
        @pl.loop(0, chunks)
        def _(step):
            w_copy(part, step).wait_recv()
            out_ref[rows_of(step), columns_of(part)] = (
                nearer[rows_of(step), columns_of(part)]
                + incoming[rows_of(step), columns_of(part)].astype(jnp.float32)
            ).astype(jnp.bfloat16)

    for part in range(parts):
        @pl.loop(0, chunks)
        def _(step):
            w_copy(part, step).wait_send()


def on_device(factors, gap_index, gap_table, pair_level, pair_shift):
    aux_rows, occ_count, virtuals = factors.shape
    columns = occ_count * virtuals
    blocks = lax.axis_size("occ")
    rows = chunk_rows_of(aux_rows)
    chunks = aux_rows // rows
    width = part_columns_of(columns)
    parts = columns // width
    scale = -1.3 / (blocks * STEPS * columns * columns)
    gradient, pair_energy = pl.pallas_call(
        functools.partial(kernel, blocks, rows, width, scale),
        out_shape=(
            OUT_SPACE((aux_rows, columns), jnp.bfloat16),
            jax.ShapeDtypeStruct((1,), jnp.float32),
        ),
        in_specs=[
            pl.BlockSpec(memory_space=pl.ANY),
            pl.BlockSpec(memory_space=pl.ANY),
            pl.BlockSpec(memory_space=pltpu.SMEM),
            pl.BlockSpec(memory_space=pltpu.SMEM),
            pl.BlockSpec(memory_space=pltpu.SMEM),
        ],
        out_specs=(
            pl.BlockSpec(memory_space=pltpu.VMEM),
            pl.BlockSpec(memory_space=pltpu.SMEM),
        ),
        scratch_shapes=[
            pltpu.VMEM((aux_rows, columns), jnp.bfloat16),
            pltpu.VMEM((aux_rows, columns), jnp.bfloat16),
            pltpu.VMEM((aux_rows, columns), jnp.bfloat16),
            pltpu.VMEM((aux_rows, columns), jnp.bfloat16),
            pltpu.VMEM((aux_rows, columns), jnp.float32),
            pltpu.VMEM((columns, columns), jnp.float32),
            pltpu.VMEM((columns, columns), jnp.float32),
            pltpu.VMEM((columns, columns), jnp.bfloat16),
            pltpu.VMEM((blocks, columns), jnp.int32),
            pltpu.VMEM((8, 128), jnp.float32),
            pltpu.VMEM((blocks, 8, 128), jnp.float32),
            pltpu.SemaphoreType.DMA,
            pltpu.SemaphoreType.DMA,
            pltpu.SemaphoreType.DMA((parts, chunks)),
            pltpu.SemaphoreType.DMA((parts, chunks)),
            pltpu.SemaphoreType.DMA((parts, chunks)),
            pltpu.SemaphoreType.DMA((parts, chunks)),
            pltpu.SemaphoreType.DMA((blocks,)),
            pltpu.SemaphoreType.DMA((blocks,)),
            pltpu.SemaphoreType.REGULAR,
            pltpu.SemaphoreType.REGULAR((max(stages_of(blocks), 1),)),
        ],
        compiler_params=pltpu.CompilerParams(
            collective_id=0, has_side_effects=True, vmem_limit_bytes=56 * 1024 * 1024
        ),
    )(
        factors.reshape(aux_rows, columns),
        gap_index.reshape(blocks, columns),
        gap_table,
        pair_level.reshape(-1),
        pair_shift,
    )
    return gradient.reshape(aux_rows, occ_count, virtuals), pair_energy


OUT_SPACE = pltpu.VMEM


def solution(mesh):
    in_specs = (P("cell", "occ", None), P("cell", None), P("cell"), P("cell", None), P())
    out_specs = (P("cell", "occ", None), P("cell"))
    return jax.shard_map(
        on_device, mesh=mesh, in_specs=in_specs, out_specs=out_specs, check_vma=False
    )
```
